32 devices in a mesh: dp: 8 (over z, y), mp: 4 (over x, core).
Axes of the slice: x: 2, y: 2, z: 4, core: 2. Of those that a mesh axis runs over, the one named last changes fastest.
Arguments:
- block_input: float32 [4096, 1024], P(('dp', 'mp')), may hold values from -12 to 12
- seq_lengths: int32 [8, 3], P('dp'), may hold values from 1 to 256, 512 in all within a row
- ln1_gain: float32 [1024], replicated, may hold values from 0.5 to 1.5
- ln1_bias: float32 [1024], replicated, may hold values from -3 to 3
- w_query: bfloat16 [1024, 1024], P('dp', 'mp'), may hold values from -0.25 to 0.25
- b_query: float32 [1024], replicated, may hold values from -3 to 3
- w_key: bfloat16 [1024, 1024], P('dp', 'mp'), may hold values from -0.25 to 0.25
- w_value: bfloat16 [1024, 1024], P('dp', 'mp'), may hold values from -0.1875 to 0.1875
- b_value: float32 [1024], replicated, may hold values from -3 to 3
- w_out: bfloat16 [1024, 1024], P('mp', 'dp'), may hold values from -0.5 to 0.5
- b_out: float32 [1024], replicated, may hold values from -3 to 3
- ln2_gain: float32 [1024], replicated, may hold values from 0.5 to 1.5
- ln2_bias: float32 [1024], replicated, may hold values from -3 to 3
- w_fc: bfloat16 [1024, 4096], P('dp', 'mp'), may hold values from -0.1875 to 0.1875
- b_fc: float32 [4096], replicated, may hold values from -3 to 3
- w_proj: bfloat16 [4096, 1024], P('mp', 'dp'), may hold values from -0.125 to 0.125
- b_proj: float32 [1024], replicated, may hold values from -3 to 3
- grad_output: float32 [4096, 1024], P(('dp', 'mp')), may hold values from -6 to 6
Outputs:
- block_output: float32 [4096, 1024], P(('dp', 'mp'))
- grad_input: float32 [4096, 1024], P(('dp', 'mp'))
- grad_ln1_gain: float32 [1024], replicated
- grad_ln1_bias: float32 [1024], replicated
- grad_w_query: float32 [1024, 1024], P('dp', 'mp')
- grad_b_query: float32 [1024], replicated
- grad_w_key: float32 [1024, 1024], P('dp', 'mp')
- grad_w_value: float32 [1024, 1024], P('dp', 'mp')
- grad_b_value: float32 [1024], replicated
- grad_w_out: float32 [1024, 1024], P('mp', 'dp')
- grad_b_out: float32 [1024], replicated
- grad_ln2_gain: float32 [1024], replicated
- grad_ln2_bias: float32 [1024], replicated
- grad_w_fc: float32 [1024, 4096], P('dp', 'mp')
- grad_b_fc: float32 [4096], replicated
- grad_w_proj: float32 [4096, 1024], P('mp', 'dp')
- grad_b_proj: float32 [1024], replicated
The draws below stay inside these ranges and needn't reach their ends.
Inputs may be any that keep to these rules, and one draw needn't show every extreme that they name: `seq_lengths`: row g holds the lengths of the 3 sequences packed one after another into data group g; each row sums to 512 and its largest entry is exactly 256.
All inputs are finite; a program needn't handle non-finite values.
Results may differ from the reference program's by a relative error of at most 0.012.
The reference program's roundings to bfloat16 on the way count: a program that leaves them out, or rounds other values in their place, can miss the bound.
Values may be sent and summed in bfloat16 or wider, within the bound.
No kernel may reach another device: no remote copies, remote signals or barrier semaphores. Data moves between devices by JAX's collectives and lax.ppermute only.
A program may use at most 128 MiB of HBM per device.

```python
import math
import jax
import jax.numpy as jnp
import numpy as np
from jax import lax

D = 1024
HEADS = 16
HEAD_DIM = 64
FF = 4096
TOK_GRP = 512
SEQS = 3
MOST = 256
TOKENS = 4096
N_DP = 8


def drawn_weight(key, offset):
    entries = jnp.clip(jax.random.normal(jax.random.fold_in(key, offset), (D, D), jnp.float32), -6.0, 6.0) * D ** (-0.5)
    return entries


def draw_w_query(key, part):
    return drawn_weight(key, 201).astype(jnp.bfloat16)


def draw_w_key(key, part):
    return drawn_weight(key, 202).astype(jnp.bfloat16)


def draw_block_input(key, part):
    values = jnp.clip(jax.random.normal(jax.random.fold_in(key, 301), (TOKENS, D), jnp.float32), -6.0, 6.0)
    return values


def shard_levels(own_key, shape, cuts, least, top_value):
    def one(dim, parts):
        heights = jax.random.uniform(jax.random.fold_in(jax.random.fold_in(own_key, 6), dim), (parts,), jnp.float32, least / len(cuts), top_value / len(cuts))
        return jnp.repeat(jnp.exp(heights), shape[dim] // parts).reshape((-1,) + (1,) * (len(shape) - dim - 1))

    loudness = one(*cuts[0])
    for cut in cuts[1:]:
        loudness = loudness * one(*cut)
    return loudness


def length_profile(count, total, bound, lean):
    weights = [(1 << 20) // math.isqrt(standing ** lean) + 1 for standing in range(2, count + 1)]
    surplus, holding = total - bound - (count - 1), [1] * (count - 1)
    while surplus > 0:
        movable = [i for i in range(count - 1) if holding[i] < bound]
        mass, left = sum([weights[i] for i in movable]), surplus
        for i in movable:
            more = min(bound - holding[i], max(1, left * weights[i] // mass), surplus)
            holding[i] = holding[i] + more
            surplus = surplus - more
    return np.array([bound] + holding)


def ragged_sizes(key, amount, total, limit, skew):
    if amount == 2:
        one = jax.random.randint(key, (), max(1, total - limit), min(limit, total - 1) + 1)
        return jnp.stack([one, total - one])
    lengths = jnp.asarray(length_profile(amount, total, limit, skew), jnp.int32)
    twos = (amount - 1) // 2
    donor, taker = lengths[1:1 + 2 * twos:2], lengths[2:2 + 2 * twos:2]
    room = jnp.minimum(donor - 1, limit - taker)
    shifted = jax.random.randint(jax.random.fold_in(key, 1), (twos,), 0, 1 << 20) % (room + 1)
    lengths = lengths.at[1:1 + 2 * twos:2].set(donor - shifted).at[2:2 + 2 * twos:2].set(taker + shifted)
    return lengths[jax.random.permutation(jax.random.fold_in(key, 2), amount)]


def bell_draw(stream_key, shape, width, limit, split=(), held_as=jnp.bfloat16):
    result = jax.random.normal(stream_key, shape, jnp.float32) * width
    if len(split) > 0:
        result = shard_levels(stream_key, shape, split, -0.22, 0.18) * result
    return jnp.clip(result, min=-limit, max=limit).astype(held_as)


def setup_inputs(seed: int = 0) -> dict:
    key_list = jax.random.split(jax.random.key(seed), 19)
    block_input = draw_block_input(jax.random.fold_in(key_list[18], 71), 0)
    seq_lengths = jax.vmap(lambda own: ragged_sizes(own, SEQS, TOK_GRP, MOST, 2))(jax.random.split(key_list[1], N_DP)).reshape((N_DP, SEQS)).astype(jnp.int32)
    ln1_gain = jnp.clip(1.0 + 0.1 * jax.random.normal(key_list[2], (D,), jnp.float32), 0.5, 1.5)
    ln1_bias = bell_draw(key_list[3], (D,), 0.5, 3.0, (), jnp.float32)
    w_query = draw_w_query(jax.random.fold_in(key_list[18], 71), 0)
    b_query = bell_draw(key_list[5], (D,), 0.5, 3.0, (), jnp.float32)
    w_key = draw_w_key(jax.random.fold_in(key_list[18], 71), 0)
    w_value = bell_draw(key_list[7], (D, D), D ** -0.5, 0.1875, ((0, 8), (1, 4)))
    b_value = bell_draw(key_list[8], (D,), 0.5, 3.0, (), jnp.float32)
    w_out = bell_draw(key_list[9], (D, D), (D // 8) ** -0.5, 0.5, ((0, 4), (1, 8)))
    b_out = bell_draw(key_list[10], (D,), 0.5, 3.0, (), jnp.float32)
    ln2_gain = jnp.clip(1.0 + 0.1 * jax.random.normal(key_list[11], (D,), jnp.float32), 0.5, 1.5)
    ln2_bias = bell_draw(key_list[12], (D,), 0.5, 3.0, (), jnp.float32)
    w_fc = bell_draw(key_list[13], (D, FF), D ** -0.5, 0.1875, ((0, 8), (1, 4)))
    b_fc = bell_draw(key_list[14], (FF,), 0.5, 3.0, (), jnp.float32)
    w_proj = bell_draw(key_list[15], (FF, D), (FF // 2) ** -0.5, 0.125, ((0, 4), (1, 8)))
    b_proj = bell_draw(key_list[16], (D,), 0.5, 3.0, (), jnp.float32)
    grad_output = bell_draw(key_list[17], (TOKENS, D), 1.0, 6.0, ((0, 32),), jnp.float32)
    return dict(block_input=block_input, seq_lengths=seq_lengths, ln1_gain=ln1_gain, ln1_bias=ln1_bias, w_query=w_query, b_query=b_query, w_key=w_key, w_value=w_value, b_value=b_value, w_out=w_out, b_out=b_out, ln2_gain=ln2_gain, ln2_bias=ln2_bias, w_fc=w_fc, b_fc=b_fc, w_proj=w_proj, b_proj=b_proj, grad_output=grad_output)


eps_norm = 1e-05
gelu_coef = 0.7978845608028654

def layer_norm(values, gain_vec, shift_vec):
    row_mean = lax.optimization_barrier(jnp.mean(values, axis=-1, keepdims=True))
    centred = values - row_mean
    row_var = lax.optimization_barrier(jnp.mean(centred * centred, axis=-1, keepdims=True))
    inv_std = lax.rsqrt(row_var + eps_norm)
    unit_rows = centred * inv_std
    return (unit_rows * gain_vec + shift_vec, unit_rows, inv_std)

def norm_back(grad_rows, unit_rows, inv_std, gain_vec):
    scaled = grad_rows * gain_vec
    first_mean = lax.optimization_barrier(jnp.mean(scaled, axis=-1, keepdims=True))
    second_mean = lax.optimization_barrier(jnp.mean(scaled * unit_rows, axis=-1, keepdims=True))
    return inv_std * (scaled - first_mean - unit_rows * second_mean)

def gelu_fwd(values):
    return 0.5 * values * (1.0 + jnp.tanh(gelu_coef * (values + 0.044715 * values * values * values)))

def gelu_slope(values):
    tanh_val = jnp.tanh(gelu_coef * (values + 0.044715 * values * values * values))
    return 0.5 * (1.0 + tanh_val) + 0.5 * values * (1.0 - tanh_val * tanh_val) * gelu_coef * (1.0 + 3.0 * 0.044715 * values * values)

def segment_mask(group_lengths, row_count):
    boundary = jnp.cumsum(group_lengths).astype(jnp.int32)
    places = jnp.arange(row_count, dtype=jnp.int32)
    segment = lax.optimization_barrier(jnp.sum((places[:, None] >= boundary[None, :]).astype(jnp.int32), axis=1))
    return (segment[:, None] == segment[None, :]) & (places[None, :] <= places[:, None])

def score_table(query_h, key_h, attn_mask):
    scores = jnp.einsum('qhd,khd->hqk', query_h.astype(jnp.float32), key_h.astype(jnp.float32)) * HEAD_DIM ** (-0.5)
    return jnp.where(attn_mask[None], scores, -1e+30)

def attend(query_h, key_h, value_h, attn_mask):
    scores = score_table(query_h, key_h, attn_mask)
    row_top = lax.optimization_barrier(jnp.max(scores, axis=-1, keepdims=True))
    log_total = row_top + jnp.log(lax.optimization_barrier(jnp.sum(jnp.exp(scores - row_top), axis=-1, keepdims=True)))
    probs = jnp.where(attn_mask[None], jnp.exp(scores - log_total), 0.0).astype(jnp.bfloat16)
    heads_out = jnp.einsum('hqk,khd->qhd', probs.astype(jnp.float32), value_h.astype(jnp.float32))
    return (heads_out.astype(jnp.bfloat16), log_total)

def attend_back(query_h, key_h, value_h, log_total, attn_mask, grad_heads):
    scores = score_table(query_h, key_h, attn_mask)
    prob_full = jnp.where(attn_mask[None], jnp.exp(scores - log_total), 0.0)
    prob_low = prob_full.astype(jnp.bfloat16).astype(jnp.float32)
    grad_wide = grad_heads.astype(jnp.float32)
    d_value = jnp.einsum('hqk,qhd->khd', prob_low, grad_wide)
    d_prob = jnp.einsum('qhd,khd->hqk', grad_wide, value_h.astype(jnp.float32))
    row_dot = lax.optimization_barrier(jnp.sum(prob_full * d_prob, axis=-1, keepdims=True))
    d_score = (prob_full * (d_prob - row_dot) * HEAD_DIM ** (-0.5)).astype(jnp.bfloat16).astype(jnp.float32)
    d_query = jnp.einsum('hqk,khd->qhd', d_score, key_h.astype(jnp.float32))
    d_key = jnp.einsum('hqk,qhd->khd', d_score, query_h.astype(jnp.float32))
    return (d_query, d_key, d_value)

def reference(block_input, seq_lengths, ln1_gain, ln1_bias, w_query, b_query, w_key, w_value, b_value, w_out, b_out, ln2_gain, ln2_bias, w_fc, b_fc, w_proj, b_proj, grad_output):
    low = jnp.bfloat16
    wide = jnp.float32
    shaped = (TOK_GRP, HEADS, HEAD_DIM)

    def one_group(carry, packed):
        rows_in, group_lengths, rows_grad = packed
        attn_mask = segment_mask(group_lengths, TOK_GRP)
        normed1, unit1, inv1 = layer_norm(rows_in, ln1_gain, ln1_bias)
        act_one = normed1.astype(low)
        query = (jnp.dot(act_one, w_query, preferred_element_type=wide) + b_query).astype(low)
        key_rows = jnp.dot(act_one, w_key, preferred_element_type=wide).astype(low)
        value_rows = (jnp.dot(act_one, w_value, preferred_element_type=wide) + b_value).astype(low)
        heads_out, log_total = attend(query.reshape(shaped), key_rows.reshape(shaped), value_rows.reshape(shaped), attn_mask)
        attended = heads_out.reshape(TOK_GRP, D)
        middle = rows_in + jnp.dot(attended, w_out, preferred_element_type=wide) + b_out
        normed2, unit2, inv2 = layer_norm(middle, ln2_gain, ln2_bias)
        act_two = normed2.astype(low)
        pre_act = jnp.dot(act_two, w_fc, preferred_element_type=wide) + b_fc
        hidden = gelu_fwd(pre_act).astype(low)
        output_rows = middle + jnp.dot(hidden, w_proj, preferred_element_type=wide) + b_proj
        grad_low = rows_grad.astype(low)
        g_proj = jnp.dot(hidden.T, grad_low, preferred_element_type=wide)
        d_pre = jnp.dot(grad_low, w_proj.T, preferred_element_type=wide) * gelu_slope(pre_act)
        d_pre_low = d_pre.astype(low)
        g_fc = jnp.dot(act_two.T, d_pre_low, preferred_element_type=wide)
        d_norm2 = jnp.dot(d_pre_low, w_fc.T, preferred_element_type=wide)
        d_middle = rows_grad + norm_back(d_norm2, unit2, inv2, ln2_gain)
        d_middle_low = d_middle.astype(low)
        g_out = jnp.dot(attended.T, d_middle_low, preferred_element_type=wide)
        d_attended = jnp.dot(d_middle_low, w_out.T, preferred_element_type=wide).astype(low)
        d_query, d_key, d_value = attend_back(query.reshape(shaped), key_rows.reshape(shaped), value_rows.reshape(shaped), log_total, attn_mask, d_attended.reshape(shaped))
        d_query = d_query.reshape(TOK_GRP, D)
        d_key = d_key.reshape(TOK_GRP, D)
        d_value = d_value.reshape(TOK_GRP, D)
        dq_low = d_query.astype(low)
        dk_low = d_key.astype(low)
        dv_low = d_value.astype(low)
        g_query = jnp.dot(act_one.T, dq_low, preferred_element_type=wide)
        g_key = jnp.dot(act_one.T, dk_low, preferred_element_type=wide)
        g_value = jnp.dot(act_one.T, dv_low, preferred_element_type=wide)
        d_norm1 = jnp.dot(dq_low, w_query.T, preferred_element_type=wide) + jnp.dot(dk_low, w_key.T, preferred_element_type=wide) + jnp.dot(dv_low, w_value.T, preferred_element_type=wide)
        d_input = d_middle + norm_back(d_norm1, unit1, inv1, ln1_gain)
        terms = (lax.optimization_barrier(jnp.sum(d_norm1 * unit1, axis=0)), lax.optimization_barrier(jnp.sum(d_norm1, axis=0)), g_query, lax.optimization_barrier(jnp.sum(d_query, axis=0)), g_key, g_value, lax.optimization_barrier(jnp.sum(d_value, axis=0)), g_out, lax.optimization_barrier(jnp.sum(d_middle, axis=0)), lax.optimization_barrier(jnp.sum(d_norm2 * unit2, axis=0)), lax.optimization_barrier(jnp.sum(d_norm2, axis=0)), g_fc, lax.optimization_barrier(jnp.sum(d_pre, axis=0)), g_proj, lax.optimization_barrier(jnp.sum(rows_grad, axis=0)))
        return (jax.tree.map(jnp.add, carry, terms), (output_rows, d_input))
    vec_d = jnp.zeros((D,), wide)
    start_carry = (vec_d, vec_d, jnp.zeros((D, D), wide), vec_d, jnp.zeros((D, D), wide), jnp.zeros((D, D), wide), vec_d, jnp.zeros((D, D), wide), vec_d, vec_d, vec_d, jnp.zeros((D, FF), wide), jnp.zeros((FF,), wide), jnp.zeros((FF, D), wide), vec_d)
    packed = (block_input.reshape(N_DP, TOK_GRP, D), seq_lengths, grad_output.reshape(N_DP, TOK_GRP, D))
    sums, stacked = lax.scan(one_group, start_carry, packed)
    outputs, d_inputs = stacked
    return (outputs.reshape(TOKENS, D), d_inputs.reshape(TOKENS, D), sums[0], sums[1], sums[2], sums[3], sums[4], sums[5], sums[6], sums[7], sums[8], sums[9], sums[10], sums[11], sums[12], sums[13], sums[14])
```

```python
import jax
import jax.numpy as jnp
from jax import lax
from jax.sharding import PartitionSpec as P

HEAD_DIM = 64

eps_norm = 1e-05
gelu_coef = 0.7978845608028654
low = jnp.bfloat16
wide = jnp.float32


def layer_norm(values, gain_vec, shift_vec):
    row_mean = jnp.mean(values, axis=-1, keepdims=True)
    centred = values - row_mean
    row_var = jnp.mean(centred * centred, axis=-1, keepdims=True)
    inv_std = lax.rsqrt(row_var + eps_norm)
    unit_rows = centred * inv_std
    return (unit_rows * gain_vec + shift_vec, unit_rows, inv_std)


def norm_back(grad_rows, unit_rows, inv_std, gain_vec):
    scaled = grad_rows * gain_vec
    first_mean = jnp.mean(scaled, axis=-1, keepdims=True)
    second_mean = jnp.mean(scaled * unit_rows, axis=-1, keepdims=True)
    return inv_std * (scaled - first_mean - unit_rows * second_mean)


def gelu_both(values):
    tanh_val = jnp.tanh(gelu_coef * (values + 0.044715 * values * values * values))
    act = 0.5 * values * (1.0 + tanh_val)
    slope = 0.5 * (1.0 + tanh_val) + 0.5 * values * (1.0 - tanh_val * tanh_val) * gelu_coef * (
        1.0 + 3.0 * 0.044715 * values * values
    )
    return act, slope


def segment_mask(group_lengths, row_count):
    boundary = jnp.cumsum(group_lengths)
    places = jnp.arange(row_count, dtype=jnp.int32)
    segment = jnp.sum((places[:, None] >= boundary[None, :]).astype(jnp.int32), axis=1)
    return (segment[:, None] == segment[None, :]) & (places[None, :] <= places[:, None])


def contract(left_op, right_op, left_dim, right_dim):
    return lax.dot_general(
        left_op,
        right_op,
        (((left_dim,), (right_dim,)), ((), ())),
        preferred_element_type=wide,
    )


def score_table(query_h, key_h, attn_mask):
    scores = jnp.einsum(
        "hqd,hkd->hqk", query_h, key_h, preferred_element_type=wide
    ) * HEAD_DIM ** (-0.5)
    return jnp.where(attn_mask[None], scores, -1e30)


def attend(query_h, key_h, value_h, attn_mask):
    scores = score_table(query_h, key_h, attn_mask)
    row_top = jnp.max(scores, axis=-1, keepdims=True)
    log_total = row_top + jnp.log(jnp.sum(jnp.exp(scores - row_top), axis=-1, keepdims=True))
    probs = jnp.where(attn_mask[None], jnp.exp(scores - log_total), 0.0).astype(low)
    heads_out = jnp.einsum("hqk,hkd->hqd", probs, value_h, preferred_element_type=wide)
    return (heads_out.astype(low), log_total)


def attend_back(query_h, key_h, value_h, log_total, attn_mask, grad_heads):
    scores = score_table(query_h, key_h, attn_mask)
    prob_full = jnp.where(attn_mask[None], jnp.exp(scores - log_total), 0.0)
    prob_low = prob_full.astype(low)
    d_value = jnp.einsum("hqk,hqd->hkd", prob_low, grad_heads, preferred_element_type=wide)
    d_prob = jnp.einsum("hqd,hkd->hqk", grad_heads, value_h, preferred_element_type=wide)
    row_dot = jnp.sum(prob_full * d_prob, axis=-1, keepdims=True)
    d_score = (prob_full * (d_prob - row_dot) * HEAD_DIM ** (-0.5)).astype(low)
    d_query = jnp.einsum("hqk,hkd->hqd", d_score, key_h, preferred_element_type=wide)
    d_key = jnp.einsum("hqk,hqd->hkd", d_score, query_h, preferred_element_type=wide)
    return (d_query, d_key, d_value)


def make_step(n_dp, n_mp):
    lo = 2 if n_dp % 2 == 0 else 1
    hi = n_dp // lo
    small_dp = hi <= 4
    mp_bits = n_mp.bit_length() - 1
    dp_bits = n_dp.bit_length() - 1
    pow_mp = n_mp == 1 << mp_bits
    pow_dp = n_dp == 1 << dp_bits

    def flip(value, axis, count, bit):
        return lax.ppermute(value, axis, [(i, i ^ bit) for i in range(count)])

    def ring(value):
        return lax.ppermute(
            value, "dp", [(i, (i // lo + 1) % hi * lo + i % lo) for i in range(n_dp)]
        )

    def rows_gather(part):
        if not pow_mp:
            return lax.all_gather(part, "mp", axis=0, tiled=True)
        index = lax.axis_index("mp")
        for b in reversed(range(mp_bits)):
            other = flip(part, "mp", n_mp, 1 << b)
            first = (index >> b) & 1 == 0
            mine = part.reshape((-1, 1, part.shape[-2], part.shape[-1])) if part.ndim > 2 else part[None, None]
            theirs = other.reshape(mine.shape)
            both = jnp.where(
                first,
                jnp.concatenate([mine, theirs], axis=1),
                jnp.concatenate([theirs, mine], axis=1),
            )
            part = both.reshape((-1,) + both.shape[2:])
        return part.reshape((-1, part.shape[-1]))

    def rows_sum(partial):
        if not pow_mp:
            return lax.psum_scatter(partial, "mp", scatter_dimension=0, tiled=True)
        index = lax.axis_index("mp")
        own = partial.shape[0] // n_mp
        part = partial.reshape((n_mp, own, partial.shape[1]))
        for b in range(mp_bits):
            view = part.reshape((-1, 2) + part.shape[1:])
            bit = (index >> b) & 1
            keep = lax.dynamic_index_in_dim(view, bit, 1, keepdims=False)
            give = lax.dynamic_index_in_dim(view, 1 - bit, 1, keepdims=False).astype(low)
            part = keep + flip(give, "mp", n_mp, 1 << b).astype(wide)
        return part[0]

    def gather_dp(shard):
        if not small_dp:
            return lax.all_gather(shard, "dp", axis=0, tiled=True)
        index = lax.axis_index("dp")
        z, y = index // lo, index % lo
        rows = shard.shape[0]
        full = jnp.zeros((n_dp * rows, shard.shape[1]), shard.dtype)
        cur = shard
        for k in range(hi):
            if k:
                cur = ring(cur)
            slot = (z - k) % hi * lo
            full = lax.dynamic_update_slice_in_dim(full, cur, (slot + y) * rows, 0)
            if lo > 1:
                other = flip(cur, "dp", n_dp, 1)
                full = lax.dynamic_update_slice_in_dim(full, other, (slot + 1 - y) * rows, 0)
        return full

    def scatter_dp(grad):
        if not small_dp:
            return lax.psum_scatter(grad, "dp", scatter_dimension=0, tiled=True)
        index = lax.axis_index("dp")
        z, y = index // lo, index % lo
        rows = grad.shape[0] // n_dp
        carried = None
        for k in range(1, hi + 1):
            slot = (z - k) % hi * lo
            part = lax.dynamic_slice_in_dim(grad, (slot + y) * rows, rows)
            if lo > 1:
                give = lax.dynamic_slice_in_dim(grad, (slot + 1 - y) * rows, rows).astype(low)
                part = part + flip(give, "dp", n_dp, 1).astype(wide)
            if carried is not None:
                part = part + carried.astype(wide)
            if k < hi:
                carried = ring(part.astype(low))
        return part

    def sum_all(value):
        if not (pow_mp and pow_dp):
            return lax.psum(value, ("dp", "mp"))
        for b in range(mp_bits):
            value = value + flip(value, "mp", n_mp, 1 << b)
        for b in range(dp_bits):
            value = value + flip(value, "dp", n_dp, 1 << b)
        return value

    def per_device(
        block_input,
        seq_lengths,
        ln1_gain,
        ln1_bias,
        w_query,
        b_query,
        w_key,
        w_value,
        b_value,
        w_out,
        b_out,
        ln2_gain,
        ln2_bias,
        w_fc,
        b_fc,
        w_proj,
        b_proj,
        grad_output,
    ):
        own_rows, width = block_input.shape
        mp_index = lax.axis_index("mp")
        whole_rows = own_rows * n_mp
        head_cols = w_query.shape[1]
        hidden_cols = w_fc.shape[1]
        heads = head_cols // HEAD_DIM

        def to_heads(value):
            return value.reshape(whole_rows, heads, HEAD_DIM).transpose(1, 0, 2)

        def from_heads(value):
            return value.transpose(1, 0, 2).reshape(whole_rows, head_cols)

        full_attn = gather_dp(jnp.concatenate([w_query, w_key, w_value, w_out.T], axis=1))
        normed1, unit1, inv1 = layer_norm(block_input, ln1_gain, ln1_bias)
        act_one = rows_gather(normed1.astype(low))
        full_fc = gather_dp(w_fc)
        grad_low = rows_gather(grad_output.astype(low))
        full_proj_t = gather_dp(w_proj.T)

        bias_query = lax.dynamic_slice_in_dim(b_query, mp_index * head_cols, head_cols)
        bias_value = lax.dynamic_slice_in_dim(b_value, mp_index * head_cols, head_cols)
        bias_fc = lax.dynamic_slice_in_dim(b_fc, mp_index * hidden_cols, hidden_cols)
        attn_mask = segment_mask(seq_lengths[0], whole_rows)
        full_qkv = full_attn[:, : 3 * head_cols]
        full_out_t = full_attn[:, 3 * head_cols :]

        qkv = contract(act_one, full_qkv, 1, 0)
        query = to_heads((qkv[:, :head_cols] + bias_query).astype(low))
        key = to_heads(qkv[:, head_cols : 2 * head_cols].astype(low))
        value = to_heads((qkv[:, 2 * head_cols :] + bias_value).astype(low))
        heads_out, log_total = attend(query, key, value, attn_mask)
        attended = from_heads(heads_out)
        middle = block_input + rows_sum(contract(attended, full_out_t, 1, 1)) + b_out
        normed2, unit2, inv2 = layer_norm(middle, ln2_gain, ln2_bias)
        act_two = rows_gather(normed2.astype(low))
        pre_act = contract(act_two, full_fc, 1, 0) + bias_fc
        act, slope = gelu_both(pre_act)
        hidden = act.astype(low)
        g_proj_t = contract(grad_low, hidden, 0, 0)
        d_pre = contract(grad_low, full_proj_t, 1, 0) * slope
        d_pre_low = d_pre.astype(low)
        d_norm2 = rows_sum(contract(d_pre_low, full_fc, 1, 1))
        g_fc = contract(act_two, d_pre_low, 0, 0)
        d_middle = grad_output + norm_back(d_norm2, unit2, inv2, ln2_gain)
        d_middle_low = rows_gather(d_middle.astype(low))
        block_output = middle + rows_sum(contract(hidden, full_proj_t, 1, 1)) + b_proj
        out_proj = scatter_dp(g_proj_t).T
        out_fc = scatter_dp(g_fc)
        d_attended = contract(d_middle_low, full_out_t, 1, 0).astype(low)
        d_query, d_key, d_value = attend_back(
            query, key, value, log_total, attn_mask, to_heads(d_attended)
        )
        d_qkv = jnp.concatenate([from_heads(d_query), from_heads(d_key), from_heads(d_value)], axis=1)
        d_qkv_low = d_qkv.astype(low)
        g_out_t = contract(d_middle_low, attended, 0, 0)
        g_qkv = contract(act_one, d_qkv_low, 0, 0)
        g_attn = scatter_dp(jnp.concatenate([g_qkv, g_out_t], axis=1))
        d_norm1 = rows_sum(contract(d_qkv_low, full_qkv, 1, 1))
        grad_input = d_middle + norm_back(d_norm1, unit1, inv1, ln1_gain)

        d_bias = jnp.sum(d_qkv, axis=0)

        def embed(part, total):
            holder = jnp.zeros((total,), wide)
            return lax.dynamic_update_slice_in_dim(holder, part, mp_index * part.shape[0], 0)

        pieces = (
            jnp.sum(d_norm1 * unit1, axis=0),
            jnp.sum(d_norm1, axis=0),
            embed(d_bias[:head_cols], b_query.shape[0]),
            embed(d_bias[2 * head_cols :], b_value.shape[0]),
            jnp.sum(d_middle, axis=0),
            jnp.sum(d_norm2 * unit2, axis=0),
            jnp.sum(d_norm2, axis=0),
            embed(jnp.sum(d_pre, axis=0), b_fc.shape[0]),
            jnp.sum(grad_output, axis=0),
        )
        summed = sum_all(jnp.concatenate(pieces))
        small, at = [], 0
        for piece in pieces:
            small.append(summed[at : at + piece.shape[0]])
            at += piece.shape[0]
        return (
            block_output,
            grad_input,
            small[0],
            small[1],
            g_attn[:, :head_cols],
            small[2],
            g_attn[:, head_cols : 2 * head_cols],
            g_attn[:, 2 * head_cols : 3 * head_cols],
            small[3],
            g_attn[:, 3 * head_cols :].T,
            small[4],
            small[5],
            small[6],
            out_fc,
            small[7],
            out_proj,
            small[8],
        )

    return per_device


def solution(mesh):
    rows, whole = P(("dp", "mp"), None), P()
    split, turned = P("dp", "mp"), P("mp", "dp")
    return jax.shard_map(
        make_step(mesh.shape["dp"], mesh.shape["mp"]),
        mesh=mesh,
        in_specs=(
            rows,
            P("dp", None),
            whole,
            whole,
            split,
            whole,
            split,
            split,
            whole,
            turned,
            whole,
            whole,
            whole,
            split,
            whole,
            turned,
            whole,
            rows,
        ),
        out_specs=(
            rows,
            rows,
            whole,
            whole,
            split,
            whole,
            split,
            split,
            whole,
            turned,
            whole,
            whole,
            whole,
            split,
            whole,
            turned,
            whole,
        ),
        check_vma=False,
    )
```

```python
from functools import reduce

import jax
import jax.numpy as jnp
from jax import lax
from jax.experimental import pallas as pl
from jax.experimental.pallas import tpu as pltpu
from jax.sharding import PartitionSpec as P


HEAD_DIM = 64

eps_norm = 1e-05
gelu_coef = 0.7978845608028654
low = jnp.bfloat16
wide = jnp.float32


def gelu_both(values):
    tanh_val = jnp.tanh(gelu_coef * (values + 0.044715 * values * values * values))
    act = 0.5 * values * (1.0 + tanh_val)
    slope = 0.5 * (1.0 + tanh_val) + 0.5 * values * (1.0 - tanh_val * tanh_val) * gelu_coef * (
        1.0 + 3.0 * 0.044715 * values * values
    )
    return act, slope


def contract(left_op, right_op, left_dim, right_dim):
    return lax.dot_general(
        left_op,
        right_op,
        (((left_dim,), (right_dim,)), ((), ())),
        preferred_element_type=wide,
    )


def unit_of(values):
    centred = values - jnp.mean(values, axis=-1, keepdims=True)
    inv_std = lax.rsqrt(jnp.mean(centred * centred, axis=-1, keepdims=True) + eps_norm)
    return centred * inv_std, inv_std


def norm_back(grad_rows, unit_rows, inv_std, gain_vec):
    scaled = grad_rows * gain_vec
    first_mean = jnp.mean(scaled, axis=-1, keepdims=True)
    second_mean = jnp.mean(scaled * unit_rows, axis=-1, keepdims=True)
    return inv_std * (scaled - first_mean - unit_rows * second_mean)


def call(body, outs, *operands, smem=0, scratch=()):
    spec = pl.BlockSpec(memory_space=pltpu.VMEM)
    scalar = pl.BlockSpec(memory_space=pltpu.SMEM)
    return pl.pallas_call(
        body,
        in_specs=[scalar] * smem + [spec] * (len(operands) - smem),
        out_specs=[spec] * len(outs),
        out_shape=[jax.ShapeDtypeStruct(*o) for o in outs],
        scratch_shapes=list(scratch),
    )(*operands)


def joined(refs):
    return jnp.concatenate([r[...] for r in refs], axis=0) if len(refs) > 1 else refs[0][...]


def column(places_ref, r, block):
    return pl.ds(pl.multiple_of(places_ref[r] * block, block), block)


def pack_attn(w_query, w_key, w_value, w_out):
    rows, cols = w_query.shape

    def body(q_ref, k_ref, v_ref, o_ref, out_ref):
        out_ref[:, :cols] = q_ref[...]
        out_ref[:, cols : 2 * cols] = k_ref[...]
        out_ref[:, 2 * cols : 3 * cols] = v_ref[...]
        out_ref[:, 3 * cols :] = o_ref[...].T

    return call(body, [((rows, 4 * cols), low)], w_query, w_key, w_value, w_out)[0]


def enter(places, values, grads, vectors):
    _, width = values.shape
    blocks = places.shape[0]
    block = width // blocks

    def body(places_ref, in_ref, grad_ref, vec_ref, x_ref, g_ref, n_ref, low_ref, v_ref):
        for r in range(blocks):
            here = slice(r * block, (r + 1) * block)
            at = column(places_ref, r, block)
            x_ref[:, here] = in_ref[:, at]
            v_ref[:, here] = vec_ref[:, at]
            taken = grad_ref[:, at]
            g_ref[:, here] = taken
            low_ref[:, here] = taken.astype(low)
        unit, _ = unit_of(x_ref[...])
        n_ref[...] = (unit * v_ref[0:1, :] + v_ref[1:2, :]).astype(low)

    outs = [(values.shape, wide), (values.shape, wide), (values.shape, low), (values.shape, low)]
    return call(body, outs + [(vectors.shape, wide)], places, values, grads, vectors, smem=1)


def fold(keep, got):
    half = keep.shape[0] // 2
    both = keep + got.astype(wide)
    return both[:half], both[half:].astype(low)


def mid_norm(rows_in, keep, got, vectors):
    shape = rows_in.shape

    def body(in_ref, keep_ref, got_ref, vec_ref, mid_ref, low_ref):
        middle = in_ref[...] + (keep_ref[...] + got_ref[...].astype(wide)) + vec_ref[2:3, :]
        mid_ref[...] = middle
        unit, _ = unit_of(middle)
        low_ref[...] = (unit * vec_ref[3:4, :] + vec_ref[4:5, :]).astype(low)

    return call(body, [(shape, wide), (shape, low)], rows_in, keep, got, vectors)


def mid_back(places, rows_grad, keep, got, middle, vectors):
    rows, width = rows_grad.shape
    blocks = places.shape[0]
    block = width // blocks

    def body(places_ref, grad_ref, keep_ref, got_ref, mid_ref, vec_ref, out_ref, low_ref, sum_ref):
        d_norm = keep_ref[...] + got_ref[...].astype(wide)
        unit, inv = unit_of(mid_ref[...])
        d_middle = grad_ref[...] + norm_back(d_norm, unit, inv, vec_ref[3:4, :])
        out_ref[...] = d_middle
        low_ref[...] = d_middle.astype(low)
        sums = (
            jnp.sum(d_middle, axis=0, keepdims=True),
            jnp.sum(d_norm * unit, axis=0, keepdims=True),
            jnp.sum(d_norm, axis=0, keepdims=True),
            jnp.sum(grad_ref[...], axis=0, keepdims=True),
        )
        for r in range(blocks):
            at = column(places_ref, r, block)
            for i, row in enumerate(sums):
                sum_ref[i : i + 1, at] = row[:, r * block : (r + 1) * block]

    shape = (rows, width)
    outs = [(shape, wide), (shape, low), ((4, width), wide)]
    return call(body, outs, places, rows_grad, keep, got, middle, vectors, smem=1)


def leave_input(places, d_middle, keep, got, rows_in, vectors):
    rows, width = d_middle.shape
    blocks = places.shape[0]
    block = width // blocks

    def body(places_ref, d_ref, keep_ref, got_ref, in_ref, vec_ref, out_ref, sum_ref):
        d_norm = keep_ref[...] + got_ref[...].astype(wide)
        unit, inv = unit_of(in_ref[...])
        grad = d_ref[...] + norm_back(d_norm, unit, inv, vec_ref[0:1, :])
        sums = (
            jnp.sum(d_norm * unit, axis=0, keepdims=True),
            jnp.sum(d_norm, axis=0, keepdims=True),
        )
        for r in range(blocks):
            here = slice(r * block, (r + 1) * block)
            at = column(places_ref, r, block)
            out_ref[:, at] = grad[:, here]
            for i, row in enumerate(sums):
                sum_ref[i : i + 1, at] = row[:, here]

    outs = [((rows, width), wide), ((2, width), wide)]
    return call(body, outs, places, d_middle, keep, got, rows_in, vectors, smem=1)


def leave_output(places, middle, keep, got, vectors):
    blocks = places.shape[0]
    block = middle.shape[1] // blocks

    def body(places_ref, mid_ref, keep_ref, got_ref, vec_ref, out_ref):
        for r in range(blocks):
            here = slice(r * block, (r + 1) * block)
            added = keep_ref[:, here] + got_ref[:, here].astype(wide)
            out_ref[:, column(places_ref, r, block)] = mid_ref[:, here] + added + vec_ref[5:6, here]

    return call(body, [(middle.shape, wide)], places, middle, keep, got, vectors, smem=1)[0]


def put_halves(at, values, keep_ref, give_ref):
    half = keep_ref.shape[0]
    if at.start < half:
        keep_ref[at, :] = values
    else:
        give_ref[at.start - half : at.stop - half, :] = values.astype(low)


def halves(rows, width):
    return [((rows // 2, width), wide), ((rows // 2, width), low)]


def row_steps(rows, most):
    step = most if rows % (2 * most) == 0 else rows // 2
    return [slice(i, i + step) for i in range(0, rows, step)]


def shift_of(first_ref, at, count):
    shape = (at.stop - at.start, count)
    row = at.start + lax.broadcasted_iota(jnp.int32, shape, 0)
    place = lax.broadcasted_iota(jnp.int32, shape, 1)
    return jnp.where((place >= first_ref[at, :]) & (place <= row), 0.0, -1e30)


SCORE_SCALE = HEAD_DIM ** (-0.5)


def attend(turns, acts, pieces, bias, first):
    rows, cols = first.shape[0], bias.shape[1] // 3
    width = acts[0].shape[1]
    heads = cols // HEAD_DIM
    n_act, count = len(acts), turns.shape[1]
    own = rows // count

    def body(turn_ref, *refs):
        act_refs, piece_refs = refs[:n_act], refs[n_act : n_act + len(pieces)]
        bias_ref, first_ref, qkv_ref, out_ref, log_ref, keep_ref, give_ref = refs[-7:]
        weights = joined(piece_refs)
        block = 0
        for a in act_refs:
            qkv = (contract(a[...], weights[:, : 3 * cols], 1, 0) + bias_ref[...]).astype(low)
            for n in range(a.shape[0] // own):
                to = pl.ds(pl.multiple_of(turn_ref[0, block] * own, own), own)
                qkv_ref[to, :] = qkv[n * own : (n + 1) * own]
                block += 1
        for i in range(count):
            at, seen = slice(i * own, (i + 1) * own), (i + 1) * own
            shift = shift_of(first_ref, at, seen)
            q = [
                (qkv_ref[at, h * HEAD_DIM : (h + 1) * HEAD_DIM] * SCORE_SCALE).astype(low)
                for h in range(heads)
            ]
            k = [qkv_ref[:seen, cols + h * HEAD_DIM : cols + (h + 1) * HEAD_DIM] for h in range(heads)]
            v = [
                qkv_ref[:seen, 2 * cols + h * HEAD_DIM : 2 * cols + (h + 1) * HEAD_DIM]
                for h in range(heads)
            ]
            scores = [contract(a, b, 1, 1) + shift for a, b in zip(q, k)]
            tops = [jnp.max(t, axis=-1, keepdims=True) for t in scores]
            parts = [jnp.exp(t - m) for t, m in zip(scores, tops)]
            totals = [jnp.sum(t, axis=-1, keepdims=True) for t in parts]
            probs = [(t * (1.0 / n)).astype(low) for t, n in zip(parts, totals)]
            outs = [contract(a, b, 1, 0).astype(low) for a, b in zip(probs, v)]
            logs = [m + jnp.log(n) for m, n in zip(tops, totals)]
            to = pl.ds(pl.multiple_of(turn_ref[1, i] * own, own), own)
            out_ref[to, :] = jnp.concatenate(outs, axis=1)
            log_ref[at, :] = jnp.concatenate(logs, axis=1)
        for at in row_steps(rows, 256):
            put_halves(at, contract(out_ref[at, :], weights[:, 3 * cols :], 1, 1), keep_ref, give_ref)

    outs = [((rows, 3 * cols), low), ((rows, cols), low), ((rows, heads), wide)]
    return call(body, outs + halves(rows, width), turns, *acts, *pieces, bias, first, smem=1)


def attend_back(turns, grads, pieces, qkv, logs, first):
    rows, cols = qkv.shape[0], qkv.shape[1] // 3
    width = grads[0].shape[1]
    heads = cols // HEAD_DIM
    n_act, count = len(grads), turns.shape[1]
    own = rows // count

    def body(turn_ref, *refs):
        act_refs, piece_refs = refs[:n_act], refs[n_act : n_act + len(pieces)]
        qkv_ref, log_ref, first_ref, out_ref, sum_ref, keep_ref, give_ref, grad_ref = refs[-8:]
        weights = joined(piece_refs)
        block = 0
        for a in act_refs:
            grad = contract(a[...], weights[:, 3 * cols :], 1, 0).astype(low)
            for n in range(a.shape[0] // own):
                to = pl.ds(pl.multiple_of(turn_ref[0, block] * own, own), own)
                grad_ref[to, :] = grad[n * own : (n + 1) * own]
                block += 1
        steps = [slice(i * own, (i + 1) * own) for i in range(count)]
        shifts = [shift_of(first_ref, at, at.stop) for at in steps]
        every = range(heads)
        dq = [[] for _ in every]
        dk, dv = [[0.0] * count for _ in every], [[0.0] * count for _ in every]
        for i, at in enumerate(steps):
            k = [qkv_ref[: at.stop, cols + h * HEAD_DIM : cols + (h + 1) * HEAD_DIM] for h in every]
            v = [qkv_ref[: at.stop, 2 * cols + h * HEAD_DIM : 2 * cols + (h + 1) * HEAD_DIM] for h in every]
            q = [(qkv_ref[at, h * HEAD_DIM : (h + 1) * HEAD_DIM] * SCORE_SCALE).astype(low) for h in every]
            g = [grad_ref[at, h * HEAD_DIM : (h + 1) * HEAD_DIM] for h in every]
            scores = [contract(q[h], k[h], 1, 1) for h in every]
            d_prob = [contract(g[h], v[h], 1, 1) for h in every]
            probs = [jnp.exp(scores[h] + shifts[i] - log_ref[at, h : h + 1]) for h in every]
            row_dot = [jnp.sum(probs[h] * d_prob[h], axis=-1, keepdims=True) for h in every]
            d_score = [(probs[h] * (d_prob[h] - row_dot[h])).astype(low) for h in every]
            more_v = [contract(g[h], probs[h].astype(low), 0, 0) for h in every]
            more_k = [contract(q[h], d_score[h], 0, 0) for h in every]
            for h in every:
                for j in range(i + 1):
                    dv[h][j] = dv[h][j] + more_v[h][:, steps[j]]
                    dk[h][j] = dk[h][j] + more_k[h][:, steps[j]]
                dq[h].append(contract(d_score[h], k[h], 1, 0) * SCORE_SCALE)
        found = [
            [jnp.concatenate(dq[h], axis=0) for h in every],
            [jnp.concatenate(dk[h], axis=1).T for h in every],
            [jnp.concatenate(dv[h], axis=1).T for h in every],
        ]
        for n in range(3):
            whole = jnp.concatenate(found[n], axis=1)
            for i, at in enumerate(steps):
                to = pl.ds(pl.multiple_of(turn_ref[1, i] * own, own), own)
                out_ref[to, n * cols : (n + 1) * cols] = whole[at].astype(low)
            sum_ref[:, n * cols : (n + 1) * cols] = jnp.sum(whole, axis=0, keepdims=True)
        for at in row_steps(rows, 256):
            put_halves(at, contract(out_ref[at, :], weights[:, : 3 * cols], 1, 1), keep_ref, give_ref)

    outs = [((rows, 3 * cols), low), ((1, 3 * cols), wide)] + halves(rows, width)
    operands = (turns, *grads, *pieces, qkv, logs, first)
    return call(body, outs, *operands, smem=1, scratch=[pltpu.VMEM((rows, cols), low)])


def hidden_of(who, acts, pieces, bias):
    rows, cols = sum(a.shape[0] for a in acts), pieces[0].shape[1]
    n_act = len(acts)

    def body(*refs):
        who_ref, refs = refs[0], refs[1:]
        act_refs, piece_refs = refs[:n_act], refs[n_act : n_act + len(pieces)]
        bias_ref, hid_ref, slope_ref = refs[-3:]
        weights = joined(piece_refs)
        bias_row = bias_ref[pl.ds(who_ref[0], 1), :]
        start = 0
        for a in act_refs:
            at = slice(start, start + a.shape[0])
            act, slope = gelu_both(contract(a[...], weights, 1, 0) + bias_row)
            hid_ref[at, :] = act.astype(low)
            slope_ref[at, :] = slope
            start += a.shape[0]

    return call(body, [((rows, cols), low), ((rows, cols), wide)], who, *acts, *pieces, bias, smem=1)


def hidden_back(grads, proj_pieces, slope, fc_pieces):
    rows, cols = slope.shape
    width = grads[0].shape[1]
    n_act, n_proj = len(grads), len(proj_pieces)

    def body(*refs):
        act_refs, proj_refs = refs[:n_act], refs[n_act : n_act + n_proj]
        slope_ref, fc_refs = refs[n_act + n_proj], refs[n_act + n_proj + 1 : -4]
        out_ref, sum_ref, keep_ref, give_ref = refs[-4:]
        proj, total, start = joined(proj_refs), 0.0, 0
        for a in act_refs:
            at = slice(start, start + a.shape[0])
            d_pre = contract(a[...], proj, 1, 0) * slope_ref[at, :]
            out_ref[at, :] = d_pre.astype(low)
            total = total + jnp.sum(d_pre, axis=0, keepdims=True)
            start += a.shape[0]
        sum_ref[...] = total
        weights = joined(fc_refs)
        for at in row_steps(rows, 256):
            put_halves(at, contract(out_ref[at, :], weights, 1, 1), keep_ref, give_ref)

    outs = [((rows, cols), low), ((1, cols), wide)] + halves(rows, width)
    return call(body, outs, *grads, *proj_pieces, slope, *fc_pieces)


def project(hidden, pieces):
    rows, width = hidden.shape[0], sum(p.shape[0] for p in pieces)

    def body(*refs):
        hid_ref, piece_refs, (keep_ref, give_ref) = refs[0], refs[1:-2], refs[-2:]
        weights = joined(piece_refs)
        for at in row_steps(rows, 256):
            put_halves(at, contract(hid_ref[at, :], weights, 1, 1), keep_ref, give_ref)

    return call(body, halves(rows, width), hidden, *pieces)


def weight_grads(pairs, spans):
    width = pairs[0][0][0].shape[1]
    total = sum(right.shape[1] for _, right in pairs)
    half = width // 2
    operands = [o for lefts, right in pairs for o in (*lefts, right)]

    def body(*refs):
        out_refs = refs[len(operands) :]
        taken, at = 0, 0
        for lefts, right in pairs:
            left = joined(refs[taken : taken + len(lefts)])
            right_rows = refs[taken + len(lefts)][...]
            taken += len(lefts) + 1
            here = slice(at, at + right.shape[1])
            at += right.shape[1]
            for n, (first, last) in enumerate(spans):
                out_refs[2 * n][:, here] = contract(left[:, half + first : half + last], right_rows, 0, 0).astype(low)
                out_refs[2 * n + 1][:, here] = contract(left[:, first:last], right_rows, 0, 0).astype(low)

    outs = [((last - first, total), low) for first, last in spans for _ in range(2)]
    return call(body, outs, *operands)


def make_step(n_dp, n_mp):
    lo = 2 if n_dp % 2 == 0 else 1
    hi = n_dp // lo
    near_dp = 1 < hi <= 4
    mp_bits = n_mp.bit_length() - 1
    dp_bits = n_dp.bit_length() - 1
    pow_dp = n_dp == 1 << dp_bits
    if n_mp != 1 << mp_bits or mp_bits == 0:
        raise ValueError("bad mp size")
    row_order = [0]
    for b in reversed(range(mp_bits)):
        row_order = row_order + [o ^ (1 << b) for o in row_order]

    def flip(value, axis, count, bit):
        return lax.ppermute(value, axis, [(i, i ^ bit) for i in range(count)])

    def shift(value, far):
        return lax.ppermute(
            value, "dp", [(i, (i // lo + far) % hi * lo + i % lo) for i in range(n_dp)]
        )

    def rows_gather(part):
        for b in reversed(range(1, mp_bits)):
            part = jnp.concatenate([part, flip(part, "mp", n_mp, 1 << b)], axis=0)
        return [part, flip(part, "mp", n_mp, 1)]

    def rows_sum(keep, give):
        got = flip(give, "mp", n_mp, 1)
        for b in range(1, mp_bits):
            keep, give = fold(keep, got)
            got = flip(give, "mp", n_mp, 1 << b)
        return keep, got

    def gather_dp(shard):
        if not near_dp:
            return [lax.all_gather(shard, "dp", axis=0, tiled=True)]
        mine = [shard] * hi
        for k in range(1, hi // 2 + 1):
            mine[k] = shift(mine[k - 1], -1)
        for k in range(hi - 1, hi // 2, -1):
            mine[k] = shift(mine[(k + 1) % hi], 1)
        theirs = [flip(p, "dp", n_dp, 1) for p in mine] if lo > 1 else []
        return mine + theirs

    def scatter_dp(pairs, cuts):
        if not near_dp or lo == 1:
            grad = jnp.concatenate(
                [contract(jnp.concatenate(left, axis=0), right, 0, 0) for left, right in pairs], axis=1
            )
            return lax.psum_scatter(grad, "dp", scatter_dimension=0, tiled=True)
        rows = pairs[0][0][0].shape[1] // n_dp
        edges = [hi * n // cuts for n in range(cuts, -1, -1)]
        spans = [(a, b) for b, a in zip(edges, edges[1:]) if a < b]
        parts = weight_grads(pairs, [(a * rows, b * rows) for a, b in spans])
        gives, keeps = parts[::2], parts[1::2]
        gots = [flip(give, "dp", n_dp, 1) for give in gives]

        def part(k, more, kind):
            i = [a <= k < b for a, b in spans].index(True)
            at = slice((k - spans[i][0]) * rows, (k - spans[i][0] + 1) * rows)
            terms = [keeps[i][at], gots[i][at]] + more
            return reduce(jnp.add, [t.astype(wide) for t in terms]).astype(kind)

        up, down = [], []
        for k in range(hi // 2, 0, -1):
            up = [shift(part(k, up, low), 1)]
        for k in range(hi // 2 + 1, hi):
            down = [shift(part(k, down, low), -1)]
        return part(0, up + down, wide)

    def sum_all(value):
        if not pow_dp:
            return lax.psum(value, ("dp", "mp"))
        for b in range(mp_bits):
            value = value + flip(value, "mp", n_mp, 1 << b)
        for b in [*range(1, dp_bits), *range(min(dp_bits, 1))]:
            value = value + flip(value, "dp", n_dp, 1 << b)
        return value

    def per_device(
        block_input,
        seq_lengths,
        ln1_gain,
        ln1_bias,
        w_query,
        b_query,
        w_key,
        w_value,
        b_value,
        w_out,
        b_out,
        ln2_gain,
        ln2_bias,
        w_fc,
        b_fc,
        w_proj,
        b_proj,
        grad_output,
    ):
        own_rows, _ = block_input.shape
        mp_index = lax.axis_index("mp")
        cols = w_query.shape[1]
        hidden_cols = w_fc.shape[1]
        index = lax.axis_index("dp")
        z, y = index // lo, index % lo
        if near_dp:
            places = jnp.stack(
                [(z + k) % hi * lo + (y + t) % lo for t in range(lo) for k in range(hi)]
            ).astype(jnp.int32)
        else:
            places = jnp.zeros((1,), jnp.int32)

        attn = gather_dp(pack_attn(w_query, w_key, w_value, w_out))
        fc = gather_dp(w_fc)
        proj = gather_dp(w_proj.T)

        vectors = jnp.stack([ln1_gain, ln1_bias, b_out, ln2_gain, ln2_bias, b_proj])
        rows_in, rows_grad, normed1, grad_own, vectors = enter(
            places, block_input, grad_output, vectors
        )
        act_one = rows_gather(normed1)
        grad_low = rows_gather(grad_own)

        def own_columns(vector, count):
            return lax.dynamic_slice_in_dim(vector, mp_index * count, count)

        bias_qkv = jnp.concatenate(
            [own_columns(b_query, cols), jnp.zeros((cols,), wide), own_columns(b_value, cols)]
        )[None]
        bias_fc = b_fc.reshape(n_mp, hidden_cols)
        who = mp_index.astype(jnp.int32)[None]
        spot = jnp.arange(own_rows * n_mp, dtype=jnp.int32)[:, None]
        first = jnp.zeros_like(spot)
        edge = jnp.int32(0)
        for n in range(seq_lengths.shape[1]):
            edge = edge + seq_lengths[0, n]
            first = jnp.where(spot >= edge, edge, first)
        came = mp_index.astype(jnp.int32) ^ jnp.array(row_order, jnp.int32)
        back = [jnp.int32(0)] * n_mp
        for r, o in enumerate(row_order):
            back = [jnp.where((mp_index ^ o) == i, r, back[i]) for i in range(n_mp)]
        turns = jnp.stack([came, jnp.stack(back).astype(jnp.int32)])

        qkv, attended, logs, keep, give = attend(turns, act_one, attn, bias_qkv, first)
        keep, got = rows_sum(keep, give)
        middle, normed2 = mid_norm(rows_in, keep, got, vectors)
        act_two = rows_gather(normed2)
        hidden, slope = hidden_of(who, act_two, fc, bias_fc)
        d_pre_low, d_bias_fc, keep, give = hidden_back(grad_low, proj, slope, fc)
        keep, got = rows_sum(keep, give)
        d_middle, d_middle_own, mid_sums = mid_back(places, rows_grad, keep, got, middle, vectors)
        d_middle_low = rows_gather(d_middle_own)
        d_qkv_low, d_bias, keep, give = attend_back(
            turns, d_middle_low, attn, qkv, logs, first
        )
        keep, got = rows_sum(keep, give)
        grad_input, in_sums = leave_input(places, d_middle, keep, got, rows_in, vectors)

        keep, give = project(hidden, proj)
        keep, got = rows_sum(keep, give)
        block_output = leave_output(places, middle, keep, got, vectors)

        out_proj = scatter_dp([(grad_low, hidden)], 2)
        out_proj = out_proj.T
        out_fc = scatter_dp([(act_two, d_pre_low)], 2)
        out_all = scatter_dp([(act_one, d_qkv_low), (d_middle_low, attended)], 4)
        out_attn = out_all[:, 3 * cols :].T

        def embed(part, total):
            holder = jnp.zeros((total,), wide)
            return lax.dynamic_update_slice_in_dim(holder, part, mp_index * part.shape[0], 0)

        pieces = [in_sums[0], in_sums[1]] + [mid_sums[i] for i in range(4)] + [
            embed(d_bias[0, :cols], b_query.shape[0]),
            embed(d_bias[0, 2 * cols :], b_value.shape[0]),
            embed(d_bias_fc[0], b_fc.shape[0]),
        ]
        summed = sum_all(jnp.concatenate(pieces))
        small, at = [], 0
        for piece in pieces:
            small.append(summed[at : at + piece.shape[0]])
            at += piece.shape[0]
        return (
            block_output,
            grad_input,
            small[0],
            small[1],
            out_all[:, :cols],
            small[6],
            out_all[:, cols : 2 * cols],
            out_all[:, 2 * cols : 3 * cols],
            small[7],
            out_attn,
            small[2],
            small[3],
            small[4],
            out_fc,
            small[8],
            out_proj,
            small[5],
        )

    return per_device


def solution(mesh):
    rows, whole = P(("dp", "mp"), None), P()
    split, turned = P("dp", "mp"), P("mp", "dp")
    return jax.shard_map(
        make_step(mesh.shape["dp"], mesh.shape["mp"]),
        mesh=mesh,
        in_specs=(
            rows,
            P("dp", None),
            whole,
            whole,
            split,
            whole,
            split,
            split,
            whole,
            turned,
            whole,
            whole,
            whole,
            split,
            whole,
            turned,
            whole,
            rows,
        ),
        out_specs=(
            rows,
            rows,
            whole,
            whole,
            split,
            whole,
            split,
            split,
            whole,
            turned,
            whole,
            whole,
            whole,
            split,
            whole,
            turned,
            whole,
        ),
        check_vma=False,
    )
```
